128 devices in a mesh: layer: 4 (over x), latent: 8 (over z, core), token: 4 (over y).
Axes of the slice: x: 4, y: 4, z: 4, core: 2. Of those that a mesh axis runs over, the one named last changes fastest.
Arguments:
- residuals: bfloat16 [4, 768, 2560], P('layer', 'token'), may hold values from -6 to 6
- enc_weight: bfloat16 [4, 2560, 8192], P('layer', None, 'latent'), may hold values from -0.125 to 0.125
- enc_bias: float32 [4, 8192], P('layer', 'latent'), may hold values from -1 to 0.5
- dec_weight: bfloat16 [4, 4, 8192, 2560], P('layer', None, 'latent', 'token'), may hold values from -0.0625 to 0.0625
- dec_bias: float32 [4, 2560], P('layer', 'token'), may hold values from -3 to 3
- targets: bfloat16 [4, 768, 2560], P('layer', 'latent', 'token'), may hold values from -6 to 6
Outputs:
- grad_dec: bfloat16 [4, 4, 8192, 2560], P('layer', None, 'latent', 'token')
- grad_enc: bfloat16 [4, 2560, 8192], P('layer', 'token', 'latent')
The draws below stay inside these ranges and needn't reach their ends.
All inputs are finite; a program needn't handle non-finite values.
Results may differ from the reference program's by a relative error of at most 0.02.
Values may be sent and summed in bfloat16 or wider, within the bound.
No kernel may reach another device: no remote copies, remote signals or barrier semaphores. Data moves between devices by JAX's collectives and lax.ppermute only.
A program may use at most 128 MiB of HBM per device.

```python
import jax
import jax.numpy as jnp
from jax import lax

D = 2560
F = 8192
L = 4
TOK_DEV = 192
TOKENS = 768
N_TOKEN = 4


def levels(rng, extent, shards, low, largest):
    gain = 1.0
    for axis_at, parts in shards:
        steps = jax.random.uniform(jax.random.fold_in(jax.random.fold_in(rng, 6), axis_at), (parts,), jnp.float32, low / len(shards), largest / len(shards))
        gain = gain * jnp.repeat(jnp.exp(steps), extent[axis_at] // parts).reshape((-1,) + (1,) * (len(extent) - 1 - axis_at))
    return gain


def noise(rng, shape, deviation, bound, cuts=(), kind=jnp.bfloat16):
    drawn = deviation * jax.random.normal(rng, shape, jnp.float32)
    if cuts:
        drawn = drawn * levels(rng, shape, cuts, -0.22, 0.18)
    return jnp.clip(drawn, -bound, bound).astype(kind)


def setup_inputs(seed: int = 0) -> dict:
    splits = jax.random.split(jax.random.key(seed), 7)
    residuals = noise(splits[0], (L, TOKENS, D), 1.0, 6.0, ((0, 4), (1, 4)))
    enc_weight = noise(splits[1], (L, D, F), D ** -0.5, 0.125, ((0, 4), (2, 8)))
    enc_bias = jnp.clip(-1.0 + 1.5 * jax.random.uniform(splits[2], (L, F), jnp.float32) ** levels(splits[2], (L, F), ((0, 4), (1, 8)), -0.2, 0.2), -1.0, 0.5)
    dec_weight = noise(splits[3], (L, L, F, D), F ** -0.5, 0.0625, ((0, 4), (2, 8), (3, 4)))
    dec_bias = noise(splits[4], (L, D), 0.5, 3.0, ((0, 4), (1, 4)), jnp.float32)
    targets = noise(splits[5], (L, TOKENS, D), 1.0, 6.0, ((0, 4), (1, 8), (2, 4)))
    return {"residuals": residuals, "enc_weight": enc_weight, "enc_bias": enc_bias, "dec_weight": dec_weight, "dec_bias": dec_bias, "targets": targets}


SQRT_HALF = 0.7071067811865476
DENSITY_NORM = 0.3989422804014327
LOSS_SCALE = 64.0


def gelu_value(values):
    return 0.5 * values * (1.0 + lax.erf(values * SQRT_HALF))


def gelu_slope(values):
    return 0.5 * (1.0 + lax.erf(values * SQRT_HALF)) + values * jnp.exp(-0.5 * values * values) * DENSITY_NORM


def reference(residuals, enc_weight, enc_bias, dec_weight, dec_bias, targets):
    tokens_all = residuals.shape[1]
    preacts = []
    latents = []
    for source in range(L):
        preact = jnp.dot(residuals[source], enc_weight[source], preferred_element_type=jnp.float32) + enc_bias[source].astype(jnp.float32)
        preacts.append(preact)
        latents.append(gelu_value(preact).astype(jnp.bfloat16))
    errors = []
    for target in range(L):
        recon = jnp.zeros((tokens_all, D), jnp.float32)
        for source in range(target + 1):
            recon = recon + jnp.dot(latents[source], dec_weight[source, target], preferred_element_type=jnp.float32)
        error = recon + dec_bias[target].astype(jnp.float32) - targets[target].astype(jnp.float32)
        errors.append((LOSS_SCALE / tokens_all * error).astype(jnp.bfloat16))
    dec_rows = []
    enc_rows = []
    for source in range(L):
        blocks = []
        d_latent = jnp.zeros((tokens_all, F), jnp.float32)
        for target in range(L):
            if target >= source:
                grad_block = lax.dot_general(latents[source], errors[target], (((0,), (0,)), ((), ())), preferred_element_type=jnp.float32)
                blocks.append(grad_block.astype(jnp.bfloat16))
                d_latent = d_latent + lax.dot_general(errors[target], dec_weight[source, target], (((1,), (1,)), ((), ())), preferred_element_type=jnp.float32)
            else:
                blocks.append(jnp.zeros((F, D), jnp.bfloat16))
        dec_rows.append(jnp.stack(blocks))
        d_preact = (d_latent * gelu_slope(preacts[source])).astype(jnp.bfloat16)
        res_blocks = residuals[source].reshape(N_TOKEN, TOK_DEV, D)
        pre_blocks = d_preact.reshape(N_TOKEN, TOK_DEV, F)
        total = jnp.zeros((D, F), jnp.float32)
        for block in range(N_TOKEN):
            part_sum = lax.dot_general(res_blocks[block], pre_blocks[block], (((0,), (0,)), ((), ())), preferred_element_type=jnp.float32)
            total = total + lax.optimization_barrier(part_sum.astype(jnp.bfloat16)).astype(jnp.float32)
        enc_rows.append(total.astype(jnp.bfloat16))
    return jnp.stack(dec_rows), jnp.stack(enc_rows)
```

```python
import jax
import jax.numpy as jnp
from jax import lax
from jax.sharding import PartitionSpec as P


SQRT_HALF = 0.7071067811865476
DENSITY_NORM = 0.3989422804014327
LOSS_SCALE = 64.0
CHUNKS = ((0, 1), (3, 2))
F32 = jnp.float32
BF16 = jnp.bfloat16


def gelu_value(values):
    return 0.5 * values * (1.0 + lax.erf(values * SQRT_HALF))


def gelu_slope(values):
    return (
        0.5 * (1.0 + lax.erf(values * SQRT_HALF))
        + values * jnp.exp(-0.5 * values * values) * DENSITY_NORM
    )


def from_ahead(value, axis, size, steps, unit=1):
    return lax.ppermute(
        value, axis, [((i + steps * unit) % size, i) for i in range(size)]
    )


def swap_cores(value, size):
    return lax.ppermute(value, "latent", [(i, i ^ 1) for i in range(size)])


def body(residuals, enc_weight, enc_bias, dec_weight, dec_bias, targets):
    layers = lax.axis_size("layer")
    n_latent = lax.axis_size("latent")
    n_token = lax.axis_size("token")
    layer = lax.axis_index("layer")
    latent = lax.axis_index("latent")
    token = lax.axis_index("token")
    core = latent % 2
    plane = latent // 2
    planes = n_latent // 2
    res = residuals[0]
    rows = res.shape[0]
    tokens_all = rows * n_token
    weight = dec_weight[0]
    wid = weight.shape[2]
    half = rows // 2
    part = half // planes

    preact = jnp.dot(res, enc_weight[0], preferred_element_type=F32) + enc_bias[0]
    latents = gelu_value(preact).astype(BF16)
    lat = {0: latents}
    for k in (1, 3, 2):
        lat[k] = from_ahead(latents, "token", n_token, k)
    own_term = dec_bias[0] - targets[0].astype(F32)
    own_shift = (plane - token) % n_token
    live = jnp.arange(layers) >= layer

    def forward(ks):
        partials = []
        lhs = jnp.concatenate([lat[k] for k in ks], axis=0)
        for m in range(layers):
            prod = jnp.dot(lhs, weight[m], preferred_element_type=F32)
            prod = jnp.where(live[m], prod, 0.0).astype(BF16)
            partials.append(prod.reshape(len(ks), 2, half, wid))
        stacked = jnp.stack(partials)
        keep = lax.dynamic_index_in_dim(stacked, core, 2, keepdims=False)
        send = lax.dynamic_index_in_dim(stacked, 1 - core, 2, keepdims=False)
        other = swap_cores(send, n_latent)
        total = keep.astype(F32) + other.astype(F32)
        mask = (jnp.arange(layers) == layer)[:, None] & (jnp.array(ks) == own_shift)[None, :]
        total = total + jnp.where(mask[:, :, None, None], own_term, 0.0)
        total = total.astype(BF16).reshape(layers, len(ks), planes, part, wid)

        def piece(s):
            return lax.dynamic_index_in_dim(total, (plane + s) % planes, 2, keepdims=False)

        summed = piece(0).astype(F32)
        for s in (1, 3, 2):
            summed = summed + from_ahead(piece(s), "latent", n_latent, planes - s, 2).astype(F32)
        summed = summed.astype(BF16)
        error = summed.astype(F32)
        for s in (1, 3, 2):
            low = 2 if s == 2 else 1
            got = from_ahead(summed[low:], "layer", layers, s).astype(F32)
            error = error + jnp.pad(got, ((low, 0), (0, 0), (0, 0), (0, 0)))
        error = jnp.where(live[:, None, None, None], LOSS_SCALE / tokens_all * error, 0.0)
        error = error.astype(BF16)
        pieces = [error] + [from_ahead(error, "latent", n_latent, s, 2) for s in range(1, planes)]
        halves = jnp.zeros((layers, len(ks), planes, part, wid), BF16)
        for s in range(planes):
            halves = lax.dynamic_update_index_in_dim(halves, pieces[s], (plane + s) % planes, 2)
        halves = halves.reshape(layers, len(ks), half, wid)
        twin = swap_cores(halves, n_latent)
        lower = jnp.where(core == 0, halves, twin)
        upper = jnp.where(core == 0, twin, halves)
        return jnp.concatenate([lower, upper], axis=2)

    errors = {}
    for ks in CHUNKS:
        full = forward(ks)
        for at, k in enumerate(ks):
            errors[k] = full[:, at]

    cols = {}
    for k in range(n_token):
        shard = lax.dynamic_slice_in_dim(res, ((token - k) % n_token) * wid, wid, 1)
        cols[k] = shard if k == 0 else from_ahead(shard, "token", n_token, k)

    d_total = None
    for ks in CHUNKS:
        err = jnp.concatenate([errors[k] for k in ks], axis=1)
        d_lat = jnp.zeros((err.shape[1], weight.shape[1]), F32)
        for m in range(layers):
            d_lat = d_lat + lax.dot_general(
                err[m], weight[m], (((1,), (1,)), ((), ())), preferred_element_type=F32
            )
        d_lat = d_lat.astype(BF16)
        for at, k in enumerate(ks):
            mine = d_lat[at * rows : (at + 1) * rows]
            if k:
                mine = from_ahead(mine, "token", n_token, n_token - k)
            mine = mine.astype(F32)
            d_total = mine if d_total is None else d_total + mine
    d_pre = (d_total * gelu_slope(preact)).astype(BF16)
    enc_total = None
    for k in (0, 1, 3, 2):
        got = d_pre if k == 0 else from_ahead(d_pre, "token", n_token, k)
        prod = lax.dot_general(cols[k], got, (((0,), (0,)), ((), ())), preferred_element_type=F32)
        enc_total = prod if enc_total is None else enc_total + prod
    grad_enc = enc_total.astype(BF16)

    order = [k for ks in CHUNKS for k in ks]
    lat_all = jnp.concatenate([lat[k] for k in order], axis=0)
    grads = []
    for m in range(layers):
        err = jnp.concatenate([errors[k][m] for k in order], axis=0)
        grads.append(
            lax.dot_general(lat_all, err, (((0,), (0,)), ((), ())), preferred_element_type=F32).astype(BF16)
        )
    return (jnp.stack(grads)[None], grad_enc[None])


def solution(mesh):
    placed = (
        P("layer", "token", None),
        P("layer", None, "latent"),
        P("layer", "latent"),
        P("layer", None, "latent", "token"),
        P("layer", "token"),
        P("layer", "latent", "token"),
    )
    return jax.shard_map(
        body,
        mesh=mesh,
        in_specs=placed,
        out_specs=(P("layer", None, "latent", "token"), P("layer", "token", "latent")),
        check_vma=False,
    )
```

```python
import jax
import jax.numpy as jnp
from jax import lax
from jax.sharding import PartitionSpec as P


SQRT_HALF = 0.7071067811865476
DENSITY_NORM = 0.3989422804014327
LOSS_SCALE = 64.0
CHAINS = ((2, 3), (0, 1))
PARTS = ((0,), (1, 2, 3))
F32 = jnp.float32
BF16 = jnp.bfloat16


def gelu_value(values):
    return 0.5 * values * (1.0 + lax.erf(values * SQRT_HALF))


def gelu_slope(values):
    return (
        0.5 * (1.0 + lax.erf(values * SQRT_HALF))
        + values * jnp.exp(-0.5 * values * values) * DENSITY_NORM
    )


def swap_cores(value, n_latent):
    return lax.ppermute(value, "latent", [(i, i ^ 1) for i in range(n_latent)])


def exchange(value, axis, flips):
    n_latent = lax.axis_size("latent")
    pairs = []
    for i in range(n_latent):
        flip = flips[i % 2]
        if axis == "plane":
            pairs.append((i, ((i // 2) ^ flip) * 2 + i % 2))
        else:
            size = lax.axis_size(axis)
            if axis == "layer":
                pairs += [(j * n_latent + i, (j ^ flip) * n_latent + i) for j in range(size)]
            else:
                pairs += [(i * size + j, i * size + (j ^ flip)) for j in range(size)]
    names = {"plane": "latent", "layer": ("layer", "latent"), "token": ("latent", "token")}[axis]
    return lax.ppermute(value, names, pairs)


SIDE_A = (1, 3)
SIDE_B = (3, 1)


def body(residuals, enc_weight, enc_bias, dec_weight, dec_bias, targets):
    layers = lax.axis_size("layer")
    n_latent = lax.axis_size("latent")
    n_token = lax.axis_size("token")
    layer = lax.axis_index("layer")
    latent = lax.axis_index("latent")
    token = lax.axis_index("token")
    core = latent % 2
    plane = latent // 2
    planes = n_latent // 2
    side_a = 1 + 2 * core
    side_b = 3 - 2 * core
    res = residuals[0]
    rows = res.shape[0]
    tokens_all = rows * n_token
    weight = dec_weight[0]
    wid = weight.shape[2]
    half = rows // 2
    part = half // planes

    def by_core(mine, twin):
        return jnp.where(core == 0, mine, twin), jnp.where(core == 0, twin, mine)

    preact = jnp.dot(res, enc_weight[0], preferred_element_type=F32) + enc_bias[0]
    latents = gelu_value(preact).astype(BF16)
    near = exchange(latents, "token", SIDE_B)
    far = exchange(jnp.stack([latents, near]), "token", SIDE_A)
    one, three = by_core(far[0], near)
    lat = {0: latents, 1: one, 2: far[1], 3: three}
    own_term = dec_bias[0] - targets[0].astype(F32)
    own_shift = plane ^ token

    products = {}
    for ks in PARTS:
        lhs = jnp.concatenate([lat[k] for k in ks], axis=0) if len(ks) > 1 else lat[ks[0]]
        for m in range(layers):
            prod = jnp.dot(lhs, weight[m], preferred_element_type=F32).astype(BF16)
            prod = prod.reshape(len(ks), 2, half, wid)
            for at, k in enumerate(ks):
                products[m, k] = prod[at]

    ks = tuple(range(n_token))

    def chain(ms):
        nk, nm = len(ks), len(ms)
        targets_of = jnp.array(ms)
        live = (targets_of >= layer)[:, None, None, None]
        stacked = jnp.stack([jnp.stack([products[m, k] for k in ks]) for m in ms])
        keep = lax.dynamic_index_in_dim(stacked, core, 2, keepdims=False)
        send = lax.dynamic_index_in_dim(stacked, 1 - core, 2, keepdims=False)
        other = swap_cores(send, n_latent)
        total = keep.astype(F32) + other.astype(F32)
        mask = (targets_of == layer)[:, None] & (jnp.array(ks) == own_shift)[None, :]
        total = total + jnp.where(mask[:, :, None, None], own_term, 0.0)
        total = jnp.where(live, total, 0.0)
        total = total.astype(BF16).reshape(nm, nk, planes, part, wid)

        def piece(at):
            return lax.dynamic_index_in_dim(total, plane ^ at, 2, keepdims=False)

        got = exchange(jnp.stack([piece(side_a), piece(2)]), "plane", SIDE_A)
        pass_on = (piece(side_b).astype(F32) + got[1].astype(F32)).astype(BF16)
        summed = piece(0).astype(F32) + got[0].astype(F32)
        summed = summed + exchange(pass_on, "plane", SIDE_B).astype(F32)
        summed = summed.astype(BF16)
        first = 1 if ms[0] == 0 else 0
        upper = summed[first:]
        upper = (upper.astype(F32) + exchange(upper, "layer", SIDE_A).astype(F32)).astype(BF16)
        error = upper.astype(F32) + exchange(upper, "layer", SIDE_B).astype(F32)
        if first:
            error = jnp.concatenate([summed[:1].astype(F32), error])
        error = jnp.where(live, LOSS_SCALE / tokens_all * error, 0.0).astype(BF16)
        halves = jnp.zeros((nm, nk, planes, part, wid), BF16)
        near = exchange(error, "plane", SIDE_B)
        far = exchange(jnp.stack([error, near]), "plane", SIDE_A)
        pieces = [(error, 0), (near, side_b), (far[0], side_a), (far[1], 2)]
        for value, at in pieces:
            halves = lax.dynamic_update_index_in_dim(halves, value, plane ^ at, 2)
        halves = halves.reshape(nm, nk * half, wid)
        twin = swap_cores(halves, n_latent)
        for i, m in enumerate(ms):
            errors[m] = (halves[i], twin[i])

    errors = {}

    def columns(value, at):
        return lax.dynamic_slice_in_dim(value, (token ^ at) * wid, wid, 1)

    def own_rows(value, of_twin):
        at = 1 - core if of_twin else core
        return lax.dynamic_slice_in_dim(value, at * half, half, 0)

    res = jnp.concatenate([own_rows(res, False), own_rows(res, True)], axis=0)
    cols_a = exchange(jnp.stack([columns(res, side_a), columns(res, 2)]), "token", SIDE_A)
    cols_b = exchange(jnp.stack([columns(res, side_b), cols_a[1]]), "token", SIDE_B)
    cols = (columns(res, 0), cols_b[0], cols_a[0], cols_b[1])
    for ms in CHAINS:
        chain(ms)

    def outer(left, right):
        return lax.dot_general(left, right, (((0,), (0,)), ((), ())), preferred_element_type=F32)

    order_m = [m for ms in CHAINS for m in ms]
    early, late = [], []
    for h in range(2):
        d_lat = None
        for m in order_m:
            prod = lax.dot_general(
                errors[m][h], weight[m], (((1,), (1,)), ((), ())), preferred_element_type=F32
            )
            d_lat = prod if d_lat is None else d_lat + prod
        d_lat = d_lat.astype(BF16).reshape(n_token, half, -1)
        got = exchange(lax.dynamic_slice_in_dim(d_lat, 1 + core, 2, 0), "token", SIDE_A)
        mine = lax.dynamic_index_in_dim(got, core, 0, keepdims=False)
        other = lax.dynamic_index_in_dim(got, 1 - core, 0, keepdims=False)
        pass_on = lax.dynamic_index_in_dim(d_lat, side_b, 0, keepdims=False)
        pass_on = (pass_on.astype(F32) + other.astype(F32)).astype(BF16)
        d_total = d_lat[0].astype(F32) + mine.astype(F32)
        d_total = d_total + exchange(pass_on, "token", SIDE_B).astype(F32)
        d_pre = (d_total * gelu_slope(own_rows(preact, h == 1))).astype(BF16)
        near = exchange(d_pre, "token", SIDE_B)
        far = exchange(jnp.stack([d_pre, near]), "token", SIDE_A)
        span = slice(h * half, (h + 1) * half)
        early += [(cols[0][span], d_pre), (cols[1][span], near)]
        late += [(cols[2][span], far[0]), (cols[3][span], far[1])]
    enc_total = None
    for terms in (early, late):
        prod = outer(*(jnp.concatenate(side, axis=0) for side in zip(*terms)))
        enc_total = prod if enc_total is None else enc_total + prod
    grad_enc = enc_total.astype(BF16)

    lat_all = jnp.concatenate([lat[k] for k in ks], axis=0)
    grads = []
    for m in range(layers):
        err = jnp.stack(by_core(*(v.reshape(n_token, half, wid) for v in errors[m])), axis=1)
        grads.append(outer(lat_all, err.reshape(tokens_all, wid)).astype(BF16))

    return (jnp.stack(grads)[None], grad_enc[None])


def solution(mesh):
    placed = (
        P("layer", "token", None),
        P("layer", None, "latent"),
        P("layer", "latent"),
        P("layer", None, "latent", "token"),
        P("layer", "token"),
        P("layer", "latent", "token"),
    )
    return jax.shard_map(
        body,
        mesh=mesh,
        in_specs=placed,
        out_specs=(P("layer", None, "latent", "token"), P("layer", "token", "latent")),
        check_vma=False,
    )
```

```python
import jax
import jax.numpy as jnp
from jax import lax
from jax.sharding import PartitionSpec as P


SQRT_HALF = 0.7071067811865476
DENSITY_NORM = 0.3989422804014327
LOSS_SCALE = 64.0
CHAINS = ((2, 3), (0, 1))
PARTS = ((0,), (1, 2, 3))
F32 = jnp.float32
BF16 = jnp.bfloat16


def gelu_value(values):
    return 0.5 * values * (1.0 + lax.erf(values * SQRT_HALF))


def gelu_slope(values):
    return (
        0.5 * (1.0 + lax.erf(values * SQRT_HALF))
        + values * jnp.exp(-0.5 * values * values) * DENSITY_NORM
    )


def swap_cores(value, n_latent):
    return lax.ppermute(value, "latent", [(i, i ^ 1) for i in range(n_latent)])


def exchange(value, axis, flips):
    n_latent = lax.axis_size("latent")
    pairs = []
    for i in range(n_latent):
        flip = flips[i % 2]
        if axis == "plane":
            pairs.append((i, ((i // 2) ^ flip) * 2 + i % 2))
        else:
            size = lax.axis_size(axis)
            if axis == "layer":
                pairs += [(j * n_latent + i, (j ^ flip) * n_latent + i) for j in range(size)]
            else:
                pairs += [(i * size + j, i * size + (j ^ flip)) for j in range(size)]
    names = {"plane": "latent", "layer": ("layer", "latent"), "token": ("latent", "token")}[axis]
    return lax.ppermute(value, names, pairs)


SIDE_A = (1, 3)
SIDE_B = (3, 1)


def body(residuals, enc_weight, enc_bias, dec_weight, dec_bias, targets):
    layers = lax.axis_size("layer")
    n_latent = lax.axis_size("latent")
    n_token = lax.axis_size("token")
    layer = lax.axis_index("layer")
    latent = lax.axis_index("latent")
    token = lax.axis_index("token")
    core = latent % 2
    plane = latent // 2
    planes = n_latent // 2
    side_a = 1 + 2 * core
    side_b = 3 - 2 * core
    res = residuals[0]
    rows = res.shape[0]
    tokens_all = rows * n_token
    weight = dec_weight[0]
    wid = weight.shape[2]
    half = rows // 2
    part = half // planes

    def by_core(mine, twin):
        return jnp.where(core == 0, mine, twin), jnp.where(core == 0, twin, mine)

    preact = jnp.dot(res, enc_weight[0], preferred_element_type=F32) + enc_bias[0]
    latents = gelu_value(preact).astype(BF16)
    near = exchange(latents, "token", SIDE_B)
    far = exchange(jnp.stack([latents, near]), "token", SIDE_A)
    one, three = by_core(far[0], near)
    lat = {0: latents, 1: one, 2: far[1], 3: three}
    own_term = dec_bias[0] - targets[0].astype(F32)
    own_shift = plane ^ token

    products = {}
    for ks in PARTS:
        lhs = jnp.concatenate([lat[k] for k in ks], axis=0) if len(ks) > 1 else lat[ks[0]]
        for m in range(layers):
            prod = jnp.dot(lhs, weight[m], preferred_element_type=F32).astype(BF16)
            prod = prod.reshape(len(ks), 2, half, wid)
            for at, k in enumerate(ks):
                products[m, k] = prod[at]

    ks = tuple(range(n_token))

    def chain(ms):
        nk, nm = len(ks), len(ms)
        targets_of = jnp.array(ms)
        live = (targets_of >= layer)[:, None, None, None]
        stacked = jnp.stack([jnp.stack([products[m, k] for k in ks]) for m in ms])
        keep = lax.dynamic_index_in_dim(stacked, core, 2, keepdims=False)
        send = lax.dynamic_index_in_dim(stacked, 1 - core, 2, keepdims=False)
        other = swap_cores(send, n_latent)
        total = keep.astype(F32) + other.astype(F32)
        mask = (targets_of == layer)[:, None] & (jnp.array(ks) == own_shift)[None, :]
        total = total + jnp.where(mask[:, :, None, None], own_term, 0.0)
        total = jnp.where(live, total, 0.0)
        total = total.astype(BF16).reshape(nm, nk, planes, part, wid)

        def piece(at):
            return lax.dynamic_index_in_dim(total, plane ^ at, 2, keepdims=False)

        got = exchange(jnp.stack([piece(side_a), piece(2)]), "plane", SIDE_A)
        pass_on = (piece(side_b).astype(F32) + got[1].astype(F32)).astype(BF16)
        summed = piece(0).astype(F32) + got[0].astype(F32)
        summed = summed + exchange(pass_on, "plane", SIDE_B).astype(F32)
        summed = summed.astype(BF16)
        first = 1 if ms[0] == 0 else 0
        upper = summed[first:]
        if max(ms) < 2:
            error = upper.astype(F32) + exchange(upper, "layer", (1, 1)).astype(F32)
        else:
            upper = (upper.astype(F32) + exchange(upper, "layer", SIDE_A).astype(F32)).astype(BF16)
            error = upper.astype(F32) + exchange(upper, "layer", SIDE_B).astype(F32)
        if first:
            error = jnp.concatenate([summed[:1].astype(F32), error])
        error = jnp.where(live, LOSS_SCALE / tokens_all * error, 0.0).astype(BF16)
        halves = jnp.zeros((nm, nk, planes, part, wid), BF16)
        near = exchange(error, "plane", SIDE_B)
        far = exchange(jnp.stack([error, near]), "plane", SIDE_A)
        pieces = [(error, 0), (near, side_b), (far[0], side_a), (far[1], 2)]
        for value, at in pieces:
            halves = lax.dynamic_update_index_in_dim(halves, value, plane ^ at, 2)
        halves = halves.reshape(nm, nk * half, wid)
        twin = swap_cores(halves, n_latent)
        for i, m in enumerate(ms):
            errors[m] = (halves[i], twin[i])

    errors = {}

    def columns(value, at):
        return lax.dynamic_slice_in_dim(value, (token ^ at) * wid, wid, 1)

    def own_rows(value, of_twin):
        at = 1 - core if of_twin else core
        return lax.dynamic_slice_in_dim(value, at * half, half, 0)

    res = jnp.concatenate([own_rows(res, False), own_rows(res, True)], axis=0)
    cols_a = exchange(jnp.stack([columns(res, side_a), columns(res, 2)]), "token", SIDE_A)
    cols_b = exchange(jnp.stack([columns(res, side_b), cols_a[1]]), "token", SIDE_B)
    cols = (columns(res, 0), cols_b[0], cols_a[0], cols_b[1])
    for ms in CHAINS:
        chain(ms)

    def outer(left, right):
        return lax.dot_general(left, right, (((0,), (0,)), ((), ())), preferred_element_type=F32)

    order_m = [m for ms in CHAINS[::-1] for m in ms]
    early, late = [], []
    for h in range(2):
        d_lat = None
        for m in order_m:
            prod = lax.dot_general(
                errors[m][h], weight[m], (((1,), (1,)), ((), ())), preferred_element_type=F32
            )
            d_lat = prod if d_lat is None else d_lat + prod
        d_lat = d_lat.astype(BF16).reshape(n_token, half, -1)
        got = exchange(lax.dynamic_slice_in_dim(d_lat, 1 + core, 2, 0), "token", SIDE_A)
        mine = lax.dynamic_index_in_dim(got, core, 0, keepdims=False)
        other = lax.dynamic_index_in_dim(got, 1 - core, 0, keepdims=False)
        pass_on = lax.dynamic_index_in_dim(d_lat, side_b, 0, keepdims=False)
        pass_on = (pass_on.astype(F32) + other.astype(F32)).astype(BF16)
        d_total = d_lat[0].astype(F32) + mine.astype(F32)
        d_total = d_total + exchange(pass_on, "token", SIDE_B).astype(F32)
        d_pre = (d_total * gelu_slope(own_rows(preact, h == 1))).astype(BF16)
        near = exchange(d_pre, "token", SIDE_B)
        far = exchange(jnp.stack([d_pre, near]), "token", SIDE_A)
        span = slice(h * half, (h + 1) * half)
        early += [(cols[0][span], d_pre), (cols[1][span], near)]
        late += [(cols[2][span], far[0]), (cols[3][span], far[1])]
    enc_total = None
    for terms in (early, late):
        prod = outer(*(jnp.concatenate(side, axis=0) for side in zip(*terms)))
        enc_total = prod if enc_total is None else enc_total + prod
    grad_enc = enc_total.astype(BF16)

    lat_all = jnp.concatenate([lat[k] for k in ks], axis=0)
    grads = []
    for m in range(layers):
        err = jnp.stack(by_core(*(v.reshape(n_token, half, wid) for v in errors[m])), axis=1)
        grads.append(outer(lat_all, err.reshape(tokens_all, wid)).astype(BF16))

    return (jnp.stack(grads)[None], grad_enc[None])


def solution(mesh):
    placed = (
        P("layer", "token", None),
        P("layer", None, "latent"),
        P("layer", "latent"),
        P("layer", None, "latent", "token"),
        P("layer", "token"),
        P("layer", "latent", "token"),
    )
    return jax.shard_map(
        body,
        mesh=mesh,
        in_specs=placed,
        out_specs=(P("layer", None, "latent", "token"), P("layer", "token", "latent")),
        check_vma=False,
    )
```

```python
import jax
import jax.numpy as jnp
from jax import lax
from jax.sharding import PartitionSpec as P


SQRT_HALF = 0.7071067811865476
DENSITY_NORM = 0.3989422804014327
LOSS_SCALE = 64.0
CHAINS = ((2, 3), (0, 1))
PARTS = ((0,), (1, 2, 3))
F32 = jnp.float32
BF16 = jnp.bfloat16


def gelu_value(values):
    return 0.5 * values * (1.0 + lax.erf(values * SQRT_HALF))


def gelu_slope(values):
    return (
        0.5 * (1.0 + lax.erf(values * SQRT_HALF))
        + values * jnp.exp(-0.5 * values * values) * DENSITY_NORM
    )


def swap_cores(value, n_latent):
    return lax.ppermute(value, "latent", [(i, i ^ 1) for i in range(n_latent)])


def exchange(value, axis, flips):
    n_latent = lax.axis_size("latent")
    pairs = []
    for i in range(n_latent):
        flip = flips[i % 2]
        if axis == "plane":
            pairs.append((i, ((i // 2) ^ flip) * 2 + i % 2))
        else:
            size = lax.axis_size(axis)
            if axis == "layer":
                pairs += [(j * n_latent + i, (j ^ flip) * n_latent + i) for j in range(size)]
            else:
                pairs += [(i * size + j, i * size + (j ^ flip)) for j in range(size)]
    names = {"plane": "latent", "layer": ("layer", "latent"), "token": ("latent", "token")}[axis]
    return lax.ppermute(value, names, pairs)


SIDE_A = (1, 3)
SIDE_B = (3, 1)


def body(residuals, enc_weight, enc_bias, dec_weight, dec_bias, targets):
    layers = lax.axis_size("layer")
    n_latent = lax.axis_size("latent")
    n_token = lax.axis_size("token")
    layer = lax.axis_index("layer")
    latent = lax.axis_index("latent")
    token = lax.axis_index("token")
    core = latent % 2
    plane = latent // 2
    planes = n_latent // 2
    side_a = 1 + 2 * core
    side_b = 3 - 2 * core
    res = residuals[0]
    rows = res.shape[0]
    tokens_all = rows * n_token
    weight = dec_weight[0]
    wid = weight.shape[2]
    half = rows // 2
    part = half // planes

    def by_core(mine, twin):
        return jnp.where(core == 0, mine, twin), jnp.where(core == 0, twin, mine)

    preact = jnp.dot(res, enc_weight[0], preferred_element_type=F32) + enc_bias[0]
    latents = gelu_value(preact).astype(BF16)
    near = exchange(latents, "token", SIDE_B)
    far = exchange(jnp.stack([latents, near]), "token", SIDE_A)
    one, three = by_core(far[0], near)
    lat = {0: latents, 1: one, 2: far[1], 3: three}
    own_term = dec_bias[0] - targets[0].astype(F32)
    own_shift = plane ^ token

    products = {}
    for ks in PARTS:
        lhs = jnp.concatenate([lat[k] for k in ks], axis=0) if len(ks) > 1 else lat[ks[0]]
        for m in range(layers):
            prod = jnp.dot(lhs, weight[m], preferred_element_type=F32).astype(BF16)
            prod = prod.reshape(len(ks), 2, half, wid)
            for at, k in enumerate(ks):
                products[m, k] = prod[at]

    ks = tuple(range(n_token))

    def chain(ms):
        nk, nm = len(ks), len(ms)
        targets_of = jnp.array(ms)
        live = (targets_of >= layer)[:, None, None, None]
        stacked = jnp.stack([jnp.stack([products[m, k] for k in ks]) for m in ms])
        keep = lax.dynamic_index_in_dim(stacked, core, 2, keepdims=False)
        send = lax.dynamic_index_in_dim(stacked, 1 - core, 2, keepdims=False)
        other = swap_cores(send, n_latent)
        total = keep.astype(F32) + other.astype(F32)
        mask = (targets_of == layer)[:, None] & (jnp.array(ks) == own_shift)[None, :]
        total = total + jnp.where(mask[:, :, None, None], own_term, 0.0)
        total = jnp.where(live, total, 0.0)
        total = total.astype(BF16).reshape(nm, nk, planes, part, wid)

        def piece(at):
            return lax.dynamic_index_in_dim(total, plane ^ at, 2, keepdims=False)

        got = exchange(jnp.stack([piece(side_a), piece(2)]), "plane", SIDE_A)
        pass_on = (piece(side_b).astype(F32) + got[1].astype(F32)).astype(BF16)
        summed = piece(0).astype(F32) + got[0].astype(F32)
        summed = summed + exchange(pass_on, "plane", SIDE_B).astype(F32)
        summed = summed.astype(BF16)
        first = 1 if ms[0] == 0 else 0
        upper = summed[first:]
        if max(ms) < 2:
            error = upper.astype(F32) + exchange(upper, "layer", (1, 1)).astype(F32)
        else:
            upper = (upper.astype(F32) + exchange(upper, "layer", SIDE_A).astype(F32)).astype(BF16)
            error = upper.astype(F32) + exchange(upper, "layer", SIDE_B).astype(F32)
        if first:
            error = jnp.concatenate([summed[:1].astype(F32), error])
        error = jnp.where(live, LOSS_SCALE / tokens_all * error, 0.0).astype(BF16)
        halves = jnp.zeros((nm, nk, planes, part, wid), BF16)
        near = exchange(error, "plane", SIDE_B)
        far = exchange(jnp.stack([error, near]), "plane", SIDE_A)
        pieces = [(error, 0), (near, side_b), (far[0], side_a), (far[1], 2)]
        for value, at in pieces:
            halves = lax.dynamic_update_index_in_dim(halves, value, plane ^ at, 2)
        halves = halves.reshape(nm, nk * half, wid)
        twin = swap_cores(halves, n_latent)
        for i, m in enumerate(ms):
            errors[m] = (halves[i], twin[i])

    errors = {}

    def columns(value, at):
        return lax.dynamic_slice_in_dim(value, (token ^ at) * wid, wid, 1)

    def own_rows(value, of_twin):
        at = 1 - core if of_twin else core
        return lax.dynamic_slice_in_dim(value, at * half, half, 0)

    res = jnp.concatenate([own_rows(res, False), own_rows(res, True)], axis=0)
    cols_a = exchange(jnp.stack([columns(res, side_a), columns(res, 2)]), "token", SIDE_A)
    cols_b = exchange(jnp.stack([columns(res, side_b), cols_a[1]]), "token", SIDE_B)
    cols = (columns(res, 0), cols_b[0], cols_a[0], cols_b[1])
    for ms in CHAINS:
        chain(ms)

    def outer(left, right):
        return lax.dot_general(left, right, (((0,), (0,)), ((), ())), preferred_element_type=F32)

    order_m = [m for ms in CHAINS[::-1] for m in ms]
    early, late = [], []
    far_cols = [
        jnp.concatenate([cols[2][h * half : (h + 1) * half], cols[3][h * half : (h + 1) * half]], axis=0)
        for h in range(2)
    ]
    for h in range(2):
        d_lat = None
        for m in order_m:
            prod = lax.dot_general(
                errors[m][h], weight[m], (((1,), (1,)), ((), ())), preferred_element_type=F32
            )
            d_lat = prod if d_lat is None else d_lat + prod
        d_lat = d_lat.astype(BF16).reshape(n_token, half, -1)
        got = exchange(lax.dynamic_slice_in_dim(d_lat, 1 + core, 2, 0), "token", SIDE_A)
        mine = lax.dynamic_index_in_dim(got, core, 0, keepdims=False)
        other = lax.dynamic_index_in_dim(got, 1 - core, 0, keepdims=False)
        pass_on = lax.dynamic_index_in_dim(d_lat, side_b, 0, keepdims=False)
        pass_on = (pass_on.astype(F32) + other.astype(F32)).astype(BF16)
        d_total = d_lat[0].astype(F32) + mine.astype(F32)
        d_total = d_total + exchange(pass_on, "token", SIDE_B).astype(F32)
        d_pre = (d_total * gelu_slope(own_rows(preact, h == 1))).astype(BF16)
        near = exchange(d_pre, "token", SIDE_B)
        far = exchange(jnp.stack([d_pre, near]), "token", SIDE_A)
        span = slice(h * half, (h + 1) * half)
        early += [(cols[0][span], d_pre), (cols[1][span], near)]
        late.append((far_cols[h], far.reshape(2 * half, -1)))
    enc_total = outer(*(jnp.concatenate(side, axis=0) for side in zip(*early)))
    for h in range(2):
        enc_total = enc_total + outer(*late[h])
    grad_enc = enc_total.astype(BF16)

    lat_all = jnp.concatenate([lat[k] for k in ks], axis=0)
    grads = []
    for m in range(layers):
        err = jnp.stack(by_core(*(v.reshape(n_token, half, wid) for v in errors[m])), axis=1)
        grads.append(outer(lat_all, err.reshape(tokens_all, wid)).astype(BF16))

    return (jnp.stack(grads)[None], grad_enc[None])


def solution(mesh):
    placed = (
        P("layer", "token", None),
        P("layer", None, "latent"),
        P("layer", "latent"),
        P("layer", None, "latent", "token"),
        P("layer", "token"),
        P("layer", "latent", "token"),
    )
    return jax.shard_map(
        body,
        mesh=mesh,
        in_specs=placed,
        out_specs=(P("layer", None, "latent", "token"), P("layer", "token", "latent")),
        check_vma=False,
    )
```
